32 devices in a mesh: facet: 8 (over z, y), col: 4 (over x, core).
Axes of the slice: x: 2, y: 2, z: 4, core: 2. Of those that a mesh axis runs over, the one named last changes fastest.
Arguments:
- prepared: bfloat16 [8, 2, 8192, 512], P('facet', None, None, 'col'), may hold values from -6 to 6
- sub_off: int32 [8, 4], P(None, 'col'), may hold values from 0 to 8191
- fac_off: int32 [8], replicated, may hold values from 0 to 511
- win_col: int32 [4, 128], replicated, may hold values from 0 to 255
- vis_weights: bfloat16 [8, 2, 512, 512], P('facet', None, None, 'col'), may hold values from -6 to 6
Outputs:
- facet_strips: bfloat16 [8, 2, 8192, 256], P('facet', None, 'col')
The draws below stay inside these ranges and needn't reach their ends.
All inputs are finite; a program needn't handle non-finite values.
Results may differ from the reference program's by a relative error of at most 0.0093.
Values may be sent and summed in bfloat16 or wider, within the bound.
A program may use at most 128 MiB of HBM per device.

```python
import math
import jax
import jax.numpy as jnp
from jax import lax

YF = 8192
XM = 128
XA = 512
CW = 128
FACETS = 8
NSUB = 8
OC = 256
N_COL = 4


def touch_ends(drawn, key, smallest, top_value):
    spot = [jax.random.randint(jax.random.fold_in(key, axis), (), 0, length) for axis, length in enumerate(drawn.shape)]
    main_axis = drawn.shape.index(max(drawn.shape))
    neighbour = spot[:main_axis] + [(spot[main_axis] + 1) % drawn.shape[main_axis]] + spot[main_axis + 1:]
    return drawn.at[tuple(spot)].set(smallest).at[tuple(neighbour)].set(top_value)


def levels(key, extent, pieces, smallest, high):
    loudness = 1.0
    for dim, blocks in pieces:
        steps = jax.random.uniform(jax.random.fold_in(jax.random.fold_in(key, 6), dim), (blocks,), jnp.float32, smallest / len(pieces), high / len(pieces))
        loudness = loudness * jnp.repeat(jnp.exp(steps), extent[dim] // blocks).reshape((-1,) + (1,) * (len(extent) - 1 - dim))
    return loudness


def centred(rng, dims, spread, reach, shards=(), held_as=jnp.bfloat16):
    values = jax.random.normal(rng, dims, jnp.float32) * spread
    if len(shards) > 0:
        values = levels(rng, dims, shards, -0.22, 0.18) * values
    return jnp.clip(values, min=-reach, max=reach).astype(held_as)


def setup_inputs(seed: int = 0) -> dict:
    splits = jax.random.split(jax.random.key(seed), 6)
    prepared = centred(splits[0], (FACETS, 2, YF, CW * N_COL), 1.0, 6.0, ((0, 8), (3, 4)))
    sub_off = touch_ends(jax.random.randint(splits[1], (NSUB, N_COL), 0, YF), jax.random.fold_in(splits[1], 1), 0, YF - 1).astype(jnp.int32)
    fac_off = touch_ends(jax.random.randint(splits[2], (FACETS,), 0, XA), jax.random.fold_in(splits[2], 1), 0, XA - 1).astype(jnp.int32)
    win_col = touch_ends(jax.random.randint(splits[3], (N_COL, CW), 0, OC), jax.random.fold_in(splits[3], 1), 0, OC - 1).astype(jnp.int32)
    vis_weights = centred(splits[4], (NSUB, 2, XA, CW * N_COL), 1.0, 6.0, ((0, 8), (3, 4)))
    return {"prepared": prepared, "sub_off": sub_off, "fac_off": fac_off, "win_col": win_col, "vis_weights": vis_weights}


def taper_curve(length):
    position = (jnp.arange(length, dtype=jnp.float32) + 0.5) / length
    return 0.3 + 0.7 * jnp.sin(math.pi * position) ** 2

def phases(row_ids, col_ids, length, sign_factor, scaling):
    products = row_ids[:, None] * col_ids[None, :] % length
    angles = 2.0 * math.pi / length * products.astype(jnp.float32)
    return (jnp.cos(angles) * scaling, sign_factor * jnp.sin(angles) * scaling)

def complex_block(real_part, imag_part):
    upper_rows = jnp.concatenate([real_part, -imag_part], axis=1)
    lower_rows = jnp.concatenate([imag_part, real_part], axis=1)
    return jnp.concatenate([upper_rows, lower_rows], axis=0).astype(jnp.bfloat16)

def small_tables(length):
    positions = jnp.arange(length, dtype=jnp.int32)
    taper_vals = taper_curve(length)
    fwd_re, fwd_im = phases(positions, positions, length, -1.0, 1.0 / math.sqrt(length))
    back_re, back_im = phases(positions, positions, length, 1.0, 1.0 / math.sqrt(length))
    forward = complex_block(fwd_re * taper_vals[None, :], fwd_im * taper_vals[None, :])
    backward = complex_block(back_re * taper_vals[:, None], back_im * taper_vals[:, None])
    return (forward, backward)

def grid_tables(length, facet_count, contrib_len):
    positions = jnp.arange(length, dtype=jnp.int32)
    fwd_re, fwd_im = phases(positions, positions, length, -1.0, 1.0 / math.sqrt(facet_count * contrib_len))
    back_re, back_im = phases(positions, positions, length, 1.0, 1.0 / math.sqrt(length))
    return (complex_block(fwd_re, fwd_im), complex_block(back_re, back_im))

def finish_map(columns, out_cols):
    frequency = jnp.arange(out_cols, dtype=jnp.int32)
    products = columns[:, None] * frequency[None, :] % out_cols
    angles = 2.0 * math.pi / out_cols * products.astype(jnp.float32)
    scaling = 1.0 / math.sqrt(2 * out_cols)
    real_part = jnp.cos(angles) * scaling
    imag_part = jnp.sin(angles) * scaling
    from_real = jnp.concatenate([real_part, imag_part], axis=1)
    from_imag = jnp.concatenate([-imag_part, real_part], axis=1)
    return jnp.stack([from_real, from_imag], axis=0).astype(jnp.bfloat16)

def apply_weights(spectrum, weights):
    spec_re = spectrum[..., 0, :, :]
    spec_im = spectrum[..., 1, :, :]
    weight_re = weights[..., 0, :, :].astype(jnp.float32)
    weight_im = weights[..., 1, :, :].astype(jnp.float32)
    joined = jnp.stack([weight_re * spec_re - weight_im * spec_im, weight_re * spec_im + weight_im * spec_re], axis=-3)
    return joined.astype(jnp.bfloat16)

def reference(prepared, sub_off, fac_off, win_col, vis_weights):
    forward_small, backward_small = small_tables(XM)
    forward_grid, backward_grid = grid_tables(XA, FACETS, XM)
    window_pos = jnp.arange(XM, dtype=jnp.int32)
    dest_rows = ((fac_off[:, None] + window_pos[None, :]) % XA).reshape(-1)

    def one_column(column):
        strips = lax.dynamic_slice_in_dim(prepared, column * CW, CW, 3)
        offsets = lax.dynamic_index_in_dim(sub_off, column, 1, keepdims=False)
        weights = lax.dynamic_slice_in_dim(vis_weights, column * CW, CW, 3)

        def one_subgrid(subgrid_item):
            first_row, weight_block = subgrid_item
            src_rows = (first_row + window_pos) % YF
            picked = strips[:, :, src_rows].reshape(FACETS, 2 * XM, CW)
            contrib = jnp.einsum('ab,fbc->fac', forward_small.astype(jnp.float32), picked.astype(jnp.float32)).astype(jnp.bfloat16)
            flat_rows = contrib.reshape(FACETS, 2, XM, CW).transpose(1, 0, 2, 3).reshape(2, FACETS * XM, CW).astype(jnp.float32)
            assembled = jnp.zeros((2, XA, CW), jnp.float32).at[:, dest_rows].add(flat_rows).astype(jnp.bfloat16)
            spectrum = jnp.dot(forward_grid, assembled.reshape(2 * XA, CW), preferred_element_type=jnp.float32).reshape(2, XA, CW)
            weighted = apply_weights(spectrum, weight_block)
            grid_image = jnp.dot(backward_grid, weighted.reshape(2 * XA, CW), preferred_element_type=jnp.float32).astype(jnp.bfloat16).reshape(2, XA, CW)
            return grid_image[:, dest_rows].reshape(2, FACETS, XM, CW).transpose(1, 0, 2, 3)
        return lax.map(one_subgrid, (offsets, weights))
    returned = lax.map(one_column, jnp.arange(N_COL, dtype=jnp.int32))
    all_rows = (sub_off[:, :, None] + window_pos[None, None, :]) % YF

    def one_facet(facet_index):
        summed = jnp.zeros((YF, 2 * OC), jnp.float32)
        for column in range(N_COL):
            back_part = returned[column, :, facet_index].reshape(NSUB, 2 * XM, CW)
            returned_terms = jnp.einsum('ab,sbc->sac', backward_small.astype(jnp.float32), back_part.astype(jnp.float32))
            returned_terms = returned_terms.reshape(NSUB, 2, XM, CW).transpose(1, 0, 2, 3).reshape(2, NSUB * XM, CW)
            accum = jnp.zeros((2, YF, CW), jnp.float32).at[:, all_rows[:, column].reshape(-1)].add(returned_terms)
            strip_sum = accum.astype(jnp.bfloat16)
            summed = summed + jnp.einsum('pyk,pkm->ym', strip_sum.astype(jnp.float32), finish_map(win_col[column], OC).astype(jnp.float32))
        return summed.astype(jnp.bfloat16).reshape(YF, 2, OC).transpose(1, 0, 2)
    return lax.map(one_facet, jnp.arange(FACETS, dtype=jnp.int32))
```

```python
import functools
import math

import jax
import jax.numpy as jnp
import numpy as np
from jax import lax
from jax.experimental import pallas as pl
from jax.experimental.pallas import tpu as pltpu
from jax.sharding import PartitionSpec as P

XM = 128
ALIGN = 16
MESH = pl.DeviceIdType.MESH
F32 = jnp.float32
BF16 = jnp.bfloat16


def dft(length, sign, scaling):
    ids = np.arange(length)
    angles = 2.0 * np.pi / length * (ids[:, None] * ids[None, :] % length)
    return np.cos(angles) * scaling, sign * np.sin(angles) * scaling


def stacked(real_part, imag_part, axis):
    return np.concatenate([real_part, imag_part], axis=axis).astype(jnp.bfloat16)


def window_tables(length):
    taper = 0.3 + 0.7 * np.sin(np.pi * (np.arange(length) + 0.5) / length) ** 2
    scaling = 1.0 / math.sqrt(length)
    fwd_re, fwd_im = dft(length, -1.0, scaling)
    back_re, back_im = dft(length, 1.0, scaling)
    forward = stacked(fwd_re * taper[None, :], fwd_im * taper[None, :], 0)
    backward = stacked(back_re * taper[:, None], back_im * taper[:, None], 1)
    return forward, backward


def mm(a, b):
    return jnp.dot(a, b, preferred_element_type=F32)


def iota(shape, dim):
    return lax.broadcasted_iota(jnp.int32, shape, dim)


def complex_mm(table, values, conj=False):
    prod = mm(table, values)
    n = prod.shape[0] // 2
    w = prod.shape[1] // 2
    rr, ri = prod[:n, :w], prod[:n, w:]
    ir, ii = prod[n:, :w], prod[n:, w:]
    if conj:
        return rr + ii, ri - ir
    return rr - ii, ri + ir


def exchange_kernel(
    nf, ncol, starts, fac, starts_row, prep, wts, fwd, qtab,
    terms, starts_all,
    pv, qv, wv, send1, recv1, acc, grid, send2,
    ld, s1, r1, s2, sx, sp, rt, ss, rs,
):
    me = lax.axis_index("facet")
    c = lax.axis_index("col")
    nx = ncol // 2
    xq, core = lax.div(c, 2), lax.rem(c, 2)
    partner = xq * 2 + 1 - core
    pow2 = nf & (nf - 1) == 0
    blocks = prep.shape[1]
    xa = wts.shape[1]
    chunks = 8
    step = blocks // chunks

    def peer(i):
        if not pow2:
            return lax.rem(me + i, nf)
        out, b = 0, 1
        while b < nf:
            mb, ib = lax.rem(lax.div(me, b), 2), lax.rem(lax.div(i, b), 2)
            out = out + b * (mb + ib - 2 * mb * ib)
            b *= 2
        return out

    def source(i):
        return peer(i) if pow2 else lax.rem(me + nf - i, nf)

    barrier = pltpu.get_barrier_semaphore()

    @pl.loop(1, nf)
    def _(i):
        pl.semaphore_signal(barrier, inc=1, device_id={"facet": peer(i)}, device_id_type=MESH)

    for i in range(1, ncol):
        pl.semaphore_signal(
            barrier, inc=1, device_id={"col": lax.rem(c + i, ncol)}, device_id_type=MESH
        )

    loads = [
        pltpu.make_async_copy(
            prep.at[:, pl.ds(k * step, step)], pv.at[:, pl.ds(k * step, step)], ld.at[k]
        )
        for k in range(chunks)
    ]
    q_load = pltpu.make_async_copy(qtab, qv, ld.at[chunks])
    w_load = pltpu.make_async_copy(wts, wv, ld.at[chunks + 1])
    own_starts = pltpu.make_async_copy(starts_row, starts_all.at[c], ld.at[chunks + 2])
    for copy in loads:
        copy.start()
    own_starts.start()
    q_load.start()
    w_load.start()

    def remote(src, dst, send, recv, **where):
        return pltpu.make_async_remote_copy(
            src_ref=src, dst_ref=dst, send_sem=send, recv_sem=recv,
            device_id=where, device_id_type=MESH,
        )

    def send_first(j):
        return remote(send1.at[j], recv1.at[me], s1.at[j], r1.at[me], facet=j)

    def recv_first(j):
        return remote(send1.at[j], recv1.at[j], s1.at[j], r1.at[j], facet=j)

    def send_second(j):
        return remote(send2.at[j], terms.at[c, me], s2.at[j], rt.at[c, me], facet=j)

    def arrival(cc, j):
        return remote(send2.at[j], terms.at[cc, j], s2.at[j], rt.at[cc, j], facet=j)

    def forward_x(src, j, q):
        return remote(
            src, terms.at[c, j], sx.at[q, j], rt.at[c, j], col=lax.rem(xq + q, nx) * 2 + core
        )

    def forward_partner(src, cc, j):
        return remote(src, terms.at[cc, j], sp.at[cc, j], rt.at[cc, j], col=partner)

    row_k = iota((XM, 2 * XM), 0)
    row_r = iota((XM, 2 * XM), 1)
    fwd_table = fwd[...]

    def contribution(j):
        start = starts[j]
        block = lax.div(start, XM)
        shift = lax.rem(start, XM)
        above = lax.rem(block + 1, blocks)
        top = jnp.concatenate([pv[0, block], pv[1, block]], axis=1)
        low = jnp.concatenate([pv[0, above], pv[1, above]], axis=1)
        pick = jnp.where(row_r == row_k + shift, 1.0, 0.0).astype(BF16)
        picked = mm(pick, jnp.concatenate([top, low], axis=0)).astype(BF16)
        re, im = complex_mm(fwd_table, picked)
        return jnp.concatenate([re, im], axis=1).astype(BF16)

    for copy in loads:
        copy.wait()
    pl.semaphore_wait(barrier, nf - 1 + ncol - 1)

    @pl.loop(1, nf)
    def _(i):
        j = peer(nf - i)
        send1[j] = contribution(j)
        send_first(j).start()

    recv1[me] = contribution(me)

    start_sends = []
    for i in range(1, ncol):
        to = lax.rem(c + i, ncol)
        start_sends.append(
            remote(starts_row, starts_all.at[c], ss.at[i], rs.at[c], col=to)
        )
        start_sends[-1].start()

    grid_r = iota((xa, XM), 0)
    grid_k = iota((xa, XM), 1)

    def place(j):
        hit = grid_r == lax.rem(fac[j] + grid_k, xa)
        return mm(jnp.where(hit, 1.0, 0.0).astype(BF16), recv1[j])

    acc[...] = place(me)

    @pl.loop(1, nf)
    def _(i):
        j = source(nf - i)
        recv_first(j).wait_recv()
        acc[...] += place(j)

    q_load.wait()
    w_load.wait()
    table = qv[...]
    spec_re, spec_im = complex_mm(table, acc[...].astype(BF16))
    w_re, w_im = wv[0].astype(F32), wv[1].astype(F32)
    weighted = jnp.concatenate(
        [w_re * spec_re - w_im * spec_im, w_re * spec_im + w_im * spec_re], axis=1
    ).astype(BF16)
    img_re, img_im = complex_mm(table, weighted, conj=True)
    gain = image_gain(nf, xa)
    grid[...] = (jnp.concatenate([img_re, img_im], axis=1) * gain).astype(BF16)

    back_k = iota((XM, xa), 0)
    back_r = iota((XM, xa), 1)

    def back(j):
        hit = back_r == lax.rem(fac[j] + back_k, xa)
        return mm(jnp.where(hit, 1.0, 0.0).astype(BF16), grid[...]).astype(BF16)

    send2[me] = back(me)
    own_copy = pltpu.make_async_copy(send2.at[me], terms.at[c, me], ld.at[chunks + 3])
    own_copy.start()
    for q in range(1, nx):
        forward_x(send2.at[me], me, q).start()
    forward_partner(send2.at[me], c, me).start()

    @pl.loop(1, nf)
    def _(i):
        j = peer(nf - i)
        send2[j] = back(j)
        send_second(j).start()

    def relay(j):
        for q in range(1, nx):
            cc = lax.rem(xq + nx - q, nx) * 2 + core
            arrival(cc, j).wait_recv()
            forward_partner(terms.at[cc, j], cc, j).start()

    @pl.loop(1, nf)
    def _(i):
        j = source(nf - i)
        arrival(c, j).wait_recv()
        for q in range(1, nx):
            forward_x(terms.at[c, j], j, q).start()
        forward_partner(terms.at[c, j], c, j).start()

        @pl.when(i == 2)
        def _():
            relay(me)

        @pl.when(i > 2)
        def _():
            relay(source(nf - i + 2))

    if nf == 2:
        relay(me)
    for i in range(max(1, nf - 2), nf):
        relay(source(nf - i))

    own_copy.wait()
    own_starts.wait()
    for i in range(1, ncol):
        start_sends[i - 1].wait_send()
        frm = lax.rem(c + ncol - i, ncol)
        remote(starts_row, starts_all.at[frm], ss.at[i], rs.at[frm], col=frm).wait_recv()

    @pl.loop(0, nf)
    def _(j):
        for q in range(nx):
            cc = lax.rem(xq + q, nx) * 2 + 1 - core
            arrival(cc, j).wait_recv()
            forward_partner(terms.at[c, j], lax.rem(xq + q, nx) * 2 + core, j).wait_send()
        for q in range(1, nx):
            forward_x(terms.at[c, j], j, q).wait_send()

    @pl.loop(1, nf)
    def _(i):
        j = peer(i)
        send_first(j).wait_send()
        send_second(j).wait_send()


def image_gain(nf, xa):
    return math.sqrt(nf * XM) / math.sqrt(xa)


def finish_kernel(
    nf, ncol, starts_all, win, bwd, fmap, terms, out, tv, acc, maps, stage, tsem, osem
):
    c = lax.axis_index("col")
    own_rows = out.shape[1]
    oc = out.shape[2]
    total = own_rows * ncol
    base = c * own_rows
    count = ncol * nf

    def offset(t):
        cc, j = lax.div(t, nf), lax.rem(t, nf)
        rel = starts_all[cc, 0, j] - base + XM
        rel = jnp.where(rel < 0, rel + total, rel)
        rel = jnp.where(rel >= total, rel - total, rel)
        return cc, j, rel

    def fetch(t, cc, j):
        return pltpu.make_async_copy(terms.at[cc, j], tv.at[t], tsem.at[t])

    @pl.loop(0, count)
    def _(t):
        cc, j, rel = offset(t)

        @pl.when(rel < own_rows + XM)
        def _():
            fetch(t, cc, j).start()

    fm = fmap[...]
    col_n = iota((oc, XM), 0)
    for k in range(ncol):
        hit = jnp.where(col_n == win[k : k + 1, :], 1.0, 0.0).astype(BF16)
        m = lax.dot_general(
            hit, fm, (((0,), (0,)), ((), ())), preferred_element_type=F32
        )
        m_re, m_im = m[:, :oc], m[:, oc:]
        upper = jnp.concatenate([m_re, m_im], axis=1)
        lower = jnp.concatenate([-m_im, m_re], axis=1)
        maps[k] = jnp.concatenate([upper, lower], axis=0).astype(BF16)

    acc[...] = jnp.zeros_like(acc)
    table = bwd[...]
    slot_r = iota((XM + ALIGN, XM), 0)
    slot_k = iota((XM + ALIGN, XM), 1)

    @pl.loop(0, count)
    def _(t):
        cc, j, rel = offset(t)

        @pl.when(rel < own_rows + XM)
        def _():
            fetch(t, cc, j).wait()
            moved = mm(jnp.where(slot_r == slot_k + lax.rem(rel, ALIGN), 1.0, 0.0).astype(BF16), table)
            moved = jnp.concatenate([moved[:, :XM], moved[:, XM:]], axis=0).astype(BF16)
            re, im = complex_mm(moved, tv[t])
            strip = jnp.concatenate([re, im], axis=1).astype(BF16)
            low = pl.multiple_of(lax.div(rel, ALIGN) * ALIGN, ALIGN)
            acc[pl.ds(low, XM + ALIGN), :] += mm(strip, maps[cc])

    chunk = own_rows // osem.shape[0]
    copies = []
    for k in range(osem.shape[0]):
        rows = pl.ds(k * chunk, chunk)
        src = pl.ds(XM + k * chunk, chunk)
        stage[0, rows, :] = acc[src, :oc].astype(BF16)
        stage[1, rows, :] = acc[src, oc:].astype(BF16)
        copy = pltpu.make_async_copy(stage.at[:, rows, :], out.at[:, rows, :], osem.at[k])
        copy.start()
        copies.append(copy)
    for copy in copies:
        copy.wait()


def body(prepared, sub_off, fac_off, win_col, vis_weights):
    nf = fac_off.shape[0]
    ncol = lax.axis_size("col")
    facet_strip = prepared[0]
    facet_len, width = facet_strip.shape[1:]
    strip_blocks = facet_strip.reshape(2, facet_len // XM, XM, width)
    weights = vis_weights[0]
    xa = weights.shape[1]
    oc = width * ncol // 2
    own_rows = facet_len // ncol
    starts = sub_off[:, 0]
    lanes = -(-nf // 128) * 128
    starts_row = jnp.broadcast_to(jnp.pad(starts, (0, lanes - nf))[None, :], (8, lanes))

    forward, backward = window_tables(XM)
    q_table = stacked(*dft(xa, -1.0, 1.0 / math.sqrt(nf * XM)), 0)
    out_map = stacked(*dft(oc, 1.0, 1.0 / math.sqrt(2 * oc)), 1)

    smem = pl.BlockSpec(memory_space=pltpu.SMEM)
    vmem = pl.BlockSpec(memory_space=pltpu.VMEM)
    hbm = pl.BlockSpec(memory_space=pl.ANY)
    dma = pltpu.SemaphoreType.DMA
    terms, starts_all = pl.pallas_call(
        functools.partial(exchange_kernel, nf, ncol),
        out_shape=(
            jax.ShapeDtypeStruct((ncol, nf, XM, 2 * width), BF16),
            jax.ShapeDtypeStruct((ncol, 8, lanes), jnp.int32),
        ),
        in_specs=[smem, smem, hbm, hbm, hbm, vmem, hbm],
        out_specs=(hbm, hbm),
        scratch_shapes=[
            pltpu.VMEM(strip_blocks.shape, BF16),
            pltpu.VMEM(q_table.shape, BF16),
            pltpu.VMEM(weights.shape, BF16),
            pltpu.VMEM((nf, XM, 2 * width), BF16),
            pltpu.VMEM((nf, XM, 2 * width), BF16),
            pltpu.VMEM((xa, 2 * width), F32),
            pltpu.VMEM((xa, 2 * width), BF16),
            pltpu.VMEM((nf, XM, 2 * width), BF16),
            dma((12,)), dma((nf,)), dma((nf,)), dma((nf,)),
            dma((ncol, nf)), dma((ncol, nf)), dma((ncol, nf)), dma((ncol,)), dma((ncol,)),
        ],
        compiler_params=pltpu.CompilerParams(collective_id=0, has_side_effects=True),
        name="exchange",
    )(starts, fac_off, starts_row, strip_blocks, weights, jnp.asarray(forward), jnp.asarray(q_table))
    out = pl.pallas_call(
        functools.partial(finish_kernel, nf, ncol),
        out_shape=jax.ShapeDtypeStruct((2, own_rows, oc), BF16),
        in_specs=[smem, vmem, vmem, vmem, hbm],
        out_specs=hbm,
        scratch_shapes=[
            pltpu.VMEM((ncol * nf, XM, 2 * width), BF16),
            pltpu.VMEM((own_rows + 2 * XM + ALIGN, 2 * oc), F32),
            pltpu.VMEM((ncol, 2 * width, 2 * oc), BF16),
            pltpu.VMEM((2, own_rows, oc), BF16),
            dma((ncol * nf,)),
            dma((4,)),
        ],
        name="finish",
    )(starts_all, win_col, jnp.asarray(backward), jnp.asarray(out_map), terms)
    return out[None]


def solution(mesh):
    in_specs = (
        P("facet", None, None, "col"),
        P(None, "col"),
        P(),
        P(),
        P("facet", None, None, "col"),
    )
    out_specs = P("facet", None, "col", None)
    return jax.shard_map(body, mesh=mesh, in_specs=in_specs, out_specs=out_specs, check_vma=False)
```

```python
import functools
import math

import jax
import jax.numpy as jnp
import numpy as np
from jax import lax
from jax.experimental import pallas as pl
from jax.experimental.pallas import tpu as pltpu
from jax.sharding import PartitionSpec as P

XM = 128
ALIGN = 16
CHUNKS = 8
OUT_CHUNKS = 8
LAG = 3
MESH = pl.DeviceIdType.MESH
F32 = jnp.float32
BF16 = jnp.bfloat16


def dft(length, sign, scaling):
    ids = np.arange(length)
    angles = 2.0 * np.pi / length * (ids[:, None] * ids[None, :] % length)
    return np.cos(angles) * scaling, sign * np.sin(angles) * scaling


def stacked(real_part, imag_part, axis):
    return np.concatenate([real_part, imag_part], axis=axis).astype(jnp.bfloat16)


def window_tables(length):
    taper = 0.3 + 0.7 * np.sin(np.pi * (np.arange(length) + 0.5) / length) ** 2
    scaling = 1.0 / math.sqrt(length)
    fwd_re, fwd_im = dft(length, -1.0, scaling)
    back_re, back_im = dft(length, 1.0, scaling)
    forward = stacked(fwd_re * taper[None, :], fwd_im * taper[None, :], 0)
    backward = stacked(back_re * taper[:, None], back_im * taper[:, None], 1)
    return forward, backward


def mm(a, b):
    return jnp.dot(a, b, preferred_element_type=F32)


def iota(shape, dim):
    return lax.broadcasted_iota(jnp.int32, shape, dim)


def one_hot(hit):
    return jnp.where(hit, 1.0, 0.0).astype(BF16)


def exchange_kernel(
    nf, ncol, starts, fac, prep, wts, fwd, bwd, win, fmap, qtab,
    terms, starts_all, maps_out,
    pv, qv, wv, send1, recv1, acc, grid, send2, ctab, maps, svec, fv, wdup,
    ld, s1, r1, s2, sx, sp, rt, ss, rs,
):
    me = lax.axis_index("facet")
    c = lax.axis_index("col")
    nx = ncol // 2
    xq, core = lax.div(c, 2), lax.rem(c, 2)
    partner = xq * 2 + 1 - core
    pow2 = nf & (nf - 1) == 0
    blocks = prep.shape[1]
    xa, width = wts.shape[1:]
    half = width // 2
    oc = fmap.shape[0]
    chunks = CHUNKS
    step = blocks // chunks

    def peer(i):
        if not pow2:
            return lax.rem(me + i, nf)
        out, b = 0, 1
        while b < nf:
            mb, ib = lax.rem(lax.div(me, b), 2), lax.rem(lax.div(i, b), 2)
            out = out + b * (mb + ib - 2 * mb * ib)
            b *= 2
        return out

    def source(i):
        return peer(i) if pow2 else lax.rem(me + nf - i, nf)

    barrier = pltpu.get_barrier_semaphore()

    @pl.loop(1, nf)
    def _(i):
        pl.semaphore_signal(barrier, inc=1, device_id={"facet": peer(i)}, device_id_type=MESH)

    for i in range(1, ncol):
        pl.semaphore_signal(
            barrier, inc=1, device_id={"col": lax.rem(c + i, ncol)}, device_id_type=MESH
        )

    loads = [
        pltpu.make_async_copy(
            prep.at[:, pl.ds(k * step, step)], pv.at[:, pl.ds(k * step, step)], ld.at[k]
        )
        for k in range(chunks)
    ]
    w_load = pltpu.make_async_copy(wts, wv, ld.at[chunks])
    q_load = pltpu.make_async_copy(qtab, qv, ld.at[chunks + 1])
    f_load = pltpu.make_async_copy(fmap, fv, ld.at[chunks + 2])
    for copy in loads:
        copy.start()
    w_load.start()
    q_load.start()
    f_load.start()

    lane = iota(svec.shape, 1)
    row = jnp.zeros(svec.shape, jnp.int32)
    svec[...] = lax.fori_loop(0, nf, lambda j, v: jnp.where(lane == j, starts[j], v), row)

    def remote(src, dst, send, recv, **where):
        return pltpu.make_async_remote_copy(
            src_ref=src, dst_ref=dst, send_sem=send, recv_sem=recv,
            device_id=where, device_id_type=MESH,
        )

    def send_first(h, j):
        return remote(send1.at[h, j], recv1.at[h, me], s1.at[h, j], r1.at[h, me], facet=j)

    def recv_first(h, j):
        return remote(send1.at[h, j], recv1.at[h, j], s1.at[h, j], r1.at[h, j], facet=j)

    def send_second(h, j):
        return remote(send2.at[h, j], terms.at[c, me, h], s2.at[h, j], rt.at[c, me, h], facet=j)

    def arrival(cc, j, h):
        return remote(send2.at[h, j], terms.at[cc, j, h], s2.at[h, j], rt.at[cc, j, h], facet=j)

    def forward_x(src, j, h, q):
        return remote(
            src, terms.at[c, j, h], sx.at[q, j, h], rt.at[c, j, h],
            col=lax.rem(xq + q, nx) * 2 + core,
        )

    def forward_partner(src, cc, j, h):
        return remote(src, terms.at[cc, j, h], sp.at[cc, j, h], rt.at[cc, j, h], col=partner)

    row_k = iota((XM, 2 * XM), 0)
    row_r = iota((XM, 2 * XM), 1)
    fwd_table = fwd[...]

    def contribution(j, dst):
        start = starts[j]
        block = lax.div(start, XM)
        shift = lax.rem(start, XM)
        above = lax.rem(block + 1, blocks)
        top = jnp.concatenate([pv[0, block], pv[1, block]], axis=1)
        low = jnp.concatenate([pv[0, above], pv[1, above]], axis=1)
        picked = mm(one_hot(row_r == row_k + shift), jnp.concatenate([top, low], axis=0))
        prod = mm(fwd_table, picked.astype(BF16))
        re = prod[:XM, :width] - prod[XM:, width:]
        im = prod[:XM, width:] + prod[XM:, :width]
        first = iota(re.shape, 1) < half
        dst[0, j] = jnp.where(first, re, pltpu.roll(im, half, 1)).astype(BF16)
        dst[1, j] = jnp.where(first, pltpu.roll(re, half, 1), im).astype(BF16)

    for copy in loads:
        copy.wait()
    pl.semaphore_wait(barrier, nf - 1 + ncol - 1)

    @pl.loop(1, nf)
    def _(i):
        j = peer(nf - i)
        contribution(j, send1)
        send_first(0, j).start()

    @pl.loop(1, nf)
    def _(i):
        send_first(1, peer(nf - i)).start()

    contribution(me, recv1)

    start_sends = []
    for i in range(1, ncol):
        to = lax.rem(c + i, ncol)
        start_sends.append(remote(svec, starts_all.at[c], ss.at[i], rs.at[c], col=to))
        start_sends[-1].start()
    own_starts = pltpu.make_async_copy(svec, starts_all.at[c], ld.at[chunks + 3])
    own_starts.start()

    turn = iota((XM, XM), 0) == lax.rem(iota((XM, XM), 1) + lax.rem(starts[me], ALIGN), XM)
    turned = mm(one_hot(turn), bwd[...]).astype(BF16)
    turned = jnp.concatenate([turned[:, :XM], turned[:, XM:]], axis=0)
    back_k = iota((XM, xa), 0)
    back_r = iota((XM, xa), 1)

    @pl.loop(0, nf)
    def _(j):
        hit = back_r == lax.rem(fac[j] + back_k, xa)
        ctab[j] = mm(turned, one_hot(hit)).astype(BF16)

    w_load.wait()
    near = iota((xa, width), 1) < half
    for p in range(2):
        w = wv[p].astype(F32)
        swapped = pltpu.roll(w, half, 1)
        wdup[0, p] = jnp.where(near, w, swapped)
        wdup[1, p] = jnp.where(near, swapped, w)

    grid_r = iota((xa, XM), 0)
    grid_k = iota((xa, XM), 1)

    def place(h, j):
        hit = grid_r == lax.rem(fac[j] + grid_k, xa)
        return mm(one_hot(hit), recv1[h, j])

    def twist(prod, conj):
        n = prod.shape[0] // 2
        crossed = pltpu.roll(prod[n:], half, 1)
        first = iota(crossed.shape, 1) < half
        minus = jnp.logical_not(first) if conj else first
        return prod[:n] + jnp.where(minus, -crossed, crossed)

    def window_maps():
        f_load.wait()
        fm = fv[...]
        col_n = iota((oc, width), 0)
        for k in range(ncol):
            m = lax.dot_general(
                one_hot(col_n == win[k : k + 1, :]), fm, (((0,), (0,)), ((), ())),
                preferred_element_type=F32,
            ).astype(BF16)
            m_re, m_im = m[:, :oc], m[:, oc:]
            upper = jnp.concatenate([m_re, m_im], axis=1)
            lower = jnp.concatenate([-m_im, m_re], axis=1)
            maps[k] = jnp.concatenate(
                [upper[:half], lower[:half], upper[half:], lower[half:]], axis=0
            )

    own_copies = []
    map_copy = pltpu.make_async_copy(maps, maps_out, ld.at[chunks + 4])
    for h in range(2):
        acc[...] = place(h, me)

        @pl.loop(1, nf)
        def _(i):
            j = source(nf - i)
            recv_first(h, j).wait_recv()
            acc[...] += place(h, j)

        if h == 0:
            q_load.wait()
        table = qv[...]
        spectrum = twist(mm(table, acc[...].astype(BF16)), False)
        crossed = wdup[h, 1] * pltpu.roll(spectrum, half, 1)
        weighted = wdup[h, 0] * spectrum + jnp.where(near, -crossed, crossed)
        image = twist(mm(table, weighted.astype(BF16)), True)
        grid[...] = (image * image_gain(nf, xa)).astype(BF16)

        def back(j):
            return twist(mm(ctab[j], grid[...]), False).astype(BF16)

        send2[h, me] = back(me)
        copy = pltpu.make_async_copy(
            send2.at[h, me], terms.at[c, me, h], ld.at[chunks + 5 + h]
        )
        copy.start()
        own_copies.append(copy)
        for q in range(1, nx):
            forward_x(send2.at[h, me], me, h, q).start()
        forward_partner(send2.at[h, me], c, me, h).start()

        @pl.loop(1, nf)
        def _(i):
            j = peer(nf - i)
            send2[h, j] = back(j)
            send_second(h, j).start()

        if h == 0:
            window_maps()
            map_copy.start()

    def relay(u):
        h, j = lax.div(u, nf), source(nf - lax.rem(u, nf))
        for q in range(1, nx):
            cc = lax.rem(xq + nx - q, nx) * 2 + core
            arrival(cc, j, h).wait_recv()
            forward_partner(terms.at[cc, j, h], cc, j, h).start()

    @pl.loop(0, 2 * nf)
    def _(u):
        h, i = lax.div(u, nf), lax.rem(u, nf)

        @pl.when(i > 0)
        def _():
            j = source(nf - i)
            arrival(c, j, h).wait_recv()
            for q in range(1, nx):
                forward_x(terms.at[c, j, h], j, h, q).start()
            forward_partner(terms.at[c, j, h], c, j, h).start()

        @pl.when(u >= LAG)
        def _():
            relay(u - LAG)

    @pl.loop(2 * nf - LAG, 2 * nf)
    def _(u):
        relay(u)

    for copy in own_copies:
        copy.wait()
    own_starts.wait()
    map_copy.wait()
    for i in range(1, ncol):
        start_sends[i - 1].wait_send()
        frm = lax.rem(c + ncol - i, ncol)
        remote(svec, starts_all.at[frm], ss.at[i], rs.at[frm], col=frm).wait_recv()

    @pl.loop(0, nf)
    def _(j):
        for h in range(2):
            for q in range(nx):
                cc = lax.rem(xq + q, nx) * 2 + 1 - core
                arrival(cc, j, h).wait_recv()
                mine = lax.rem(xq + q, nx) * 2 + core
                forward_partner(terms.at[c, j, h], mine, j, h).wait_send()
            for q in range(1, nx):
                forward_x(terms.at[c, j, h], j, h, q).wait_send()

    @pl.loop(1, nf)
    def _(i):
        j = peer(i)
        for h in range(2):
            send_first(h, j).wait_send()
            send_second(h, j).wait_send()


def image_gain(nf, xa):
    return math.sqrt(nf * XM) / math.sqrt(xa)


def finish_kernel(nf, ncol, starts_all, terms, maps_in, out, tv, acc, maps, stage, tsem, osem):
    c = lax.axis_index("col")
    own_rows = out.shape[1]
    oc = out.shape[2]
    total = own_rows * ncol
    base = c * own_rows
    count = ncol * nf

    def offset(t):
        cc, j = lax.div(t, nf), lax.rem(t, nf)
        rel = starts_all[cc, 0, j] - base + XM
        rel = jnp.where(rel < 0, rel + total, rel)
        rel = jnp.where(rel >= total, rel - total, rel)
        return cc, j, rel

    def fetch(t, cc, j):
        return pltpu.make_async_copy(terms.at[cc, j], tv.at[t], tsem.at[t])

    map_load = pltpu.make_async_copy(maps_in, maps, tsem.at[count])
    map_load.start()

    @pl.loop(0, count)
    def _(t):
        cc, j, rel = offset(t)

        @pl.when(rel < own_rows + XM)
        def _():
            fetch(t, cc, j).start()

    acc[...] = jnp.zeros_like(acc)
    slot = iota((XM, 2 * oc), 0)
    edge = iota((ALIGN, 2 * oc), 0)
    map_load.wait()

    @pl.loop(0, count)
    def _(t):
        cc, j, rel = offset(t)

        @pl.when(rel < own_rows + XM)
        def _():
            fetch(t, cc, j).wait()
            value = mm(jnp.concatenate([tv[t, 0], tv[t, 1]], axis=1), maps[cc])
            turn = lax.rem(rel, ALIGN)
            low = pl.multiple_of(rel - turn, ALIGN)
            acc[pl.ds(low, XM), :] += jnp.where(slot >= turn, value, 0.0)
            acc[pl.ds(pl.multiple_of(low + XM, ALIGN), ALIGN), :] += jnp.where(
                edge < turn, value[:ALIGN], 0.0
            )

    chunk = own_rows // OUT_CHUNKS
    copies = []
    for k in range(OUT_CHUNKS):
        rows = pl.ds(k * chunk, chunk)
        src = pl.ds(XM + k * chunk, chunk)
        stage[0, rows, :] = acc[src, :oc].astype(BF16)
        stage[1, rows, :] = acc[src, oc:].astype(BF16)
        copy = pltpu.make_async_copy(stage.at[:, rows, :], out.at[:, rows, :], osem.at[k])
        copy.start()
        copies.append(copy)
    for copy in copies:
        copy.wait()


def body(prepared, sub_off, fac_off, win_col, vis_weights):
    nf = fac_off.shape[0]
    ncol = lax.axis_size("col")
    facet_strip = prepared[0]
    facet_len, width = facet_strip.shape[1:]
    strip_blocks = facet_strip.reshape(2, facet_len // XM, XM, width)
    weights = vis_weights[0]
    xa = weights.shape[1]
    oc = width * ncol // 2
    own_rows = facet_len // ncol
    starts = sub_off[:, 0]
    lanes = -(-nf // 128) * 128

    forward, backward = window_tables(XM)
    q_table = stacked(*dft(xa, -1.0, 1.0 / math.sqrt(nf * XM)), 0)
    out_map = stacked(*dft(oc, 1.0, 1.0 / math.sqrt(2 * oc)), 1)

    smem = pl.BlockSpec(memory_space=pltpu.SMEM)
    vmem = pl.BlockSpec(memory_space=pltpu.VMEM)
    hbm = pl.BlockSpec(memory_space=pl.ANY)
    dma = pltpu.SemaphoreType.DMA
    halves = pltpu.VMEM((2, nf, XM, width), BF16)
    maps = (ncol, 2 * width, 2 * oc)
    terms, starts_all, maps_all = pl.pallas_call(
        functools.partial(exchange_kernel, nf, ncol),
        out_shape=(
            jax.ShapeDtypeStruct((ncol, nf, 2, XM, width), BF16),
            jax.ShapeDtypeStruct((ncol, 8, lanes), jnp.int32),
            jax.ShapeDtypeStruct(maps, BF16),
        ),
        in_specs=[smem, smem, hbm, hbm, vmem, vmem, vmem, hbm, hbm],
        out_specs=(hbm, hbm, hbm),
        scratch_shapes=[
            pltpu.VMEM(strip_blocks.shape, BF16),
            pltpu.VMEM(q_table.shape, BF16),
            pltpu.VMEM(weights.shape, BF16),
            halves,
            halves,
            pltpu.VMEM((xa, width), F32),
            pltpu.VMEM((xa, width), BF16),
            halves,
            pltpu.VMEM((nf, 2 * XM, xa), BF16),
            pltpu.VMEM(maps, BF16),
            pltpu.VMEM((8, lanes), jnp.int32),
            pltpu.VMEM(out_map.shape, BF16),
            pltpu.VMEM((2, 2, xa, width), F32),
            dma((CHUNKS + 7,)), dma((2, nf)), dma((2, nf)), dma((2, nf)),
            dma((ncol, nf, 2)), dma((ncol, nf, 2)), dma((ncol, nf, 2)), dma((ncol,)), dma((ncol,)),
        ],
        compiler_params=pltpu.CompilerParams(collective_id=0, has_side_effects=True),
        name="exchange",
    )(
        starts, fac_off, strip_blocks, weights, jnp.asarray(forward), jnp.asarray(backward),
        win_col, jnp.asarray(out_map), jnp.asarray(q_table),
    )
    out = pl.pallas_call(
        functools.partial(finish_kernel, nf, ncol),
        out_shape=jax.ShapeDtypeStruct((2, own_rows, oc), BF16),
        in_specs=[smem, hbm, hbm],
        out_specs=hbm,
        scratch_shapes=[
            pltpu.VMEM((ncol * nf, 2, XM, width), BF16),
            pltpu.VMEM((own_rows + 2 * XM + ALIGN, 2 * oc), F32),
            pltpu.VMEM(maps, BF16),
            pltpu.VMEM((2, own_rows, oc), BF16),
            dma((ncol * nf + 1,)),
            dma((OUT_CHUNKS,)),
        ],
        name="finish",
    )(starts_all, terms, maps_all)
    return out[None]


def solution(mesh):
    in_specs = (
        P("facet", None, None, "col"),
        P(None, "col"),
        P(),
        P(),
        P("facet", None, None, "col"),
    )
    out_specs = P("facet", None, "col", None)
    return jax.shard_map(body, mesh=mesh, in_specs=in_specs, out_specs=out_specs, check_vma=False)
```

```python
import functools
import math

import jax
import jax.numpy as jnp
import numpy as np
from jax import lax
from jax.experimental import pallas as pl
from jax.experimental.pallas import tpu as pltpu
from jax.sharding import PartitionSpec as P

XM = 128
ALIGN = 16
CHUNKS = 8
OUT_CHUNKS = 8
LAG = 8
MESH = pl.DeviceIdType.MESH
F32 = jnp.float32
BF16 = jnp.bfloat16


def dft(length, sign, scaling):
    ids = np.arange(length)
    angles = 2.0 * np.pi / length * (ids[:, None] * ids[None, :] % length)
    return np.cos(angles) * scaling, sign * np.sin(angles) * scaling


def stacked(real_part, imag_part, axis):
    return np.concatenate([real_part, imag_part], axis=axis).astype(jnp.bfloat16)


def window_tables(length):
    taper = 0.3 + 0.7 * np.sin(np.pi * (np.arange(length) + 0.5) / length) ** 2
    scaling = 1.0 / math.sqrt(length)
    fwd_re, fwd_im = dft(length, -1.0, scaling)
    back_re, back_im = dft(length, 1.0, scaling)
    forward = stacked(fwd_re * taper[None, :], fwd_im * taper[None, :], 0)
    backward = stacked(back_re * taper[:, None], back_im * taper[:, None], 1)
    return forward, backward


def mm(a, b):
    return jnp.dot(a, b, preferred_element_type=F32)


def iota(shape, dim):
    return lax.broadcasted_iota(jnp.int32, shape, dim)


def one_hot(hit):
    return jnp.where(hit, 1.0, 0.0).astype(BF16)


def exchange_kernel(
    nf, ncol, starts, fac, prep, wts, fwd, bwd, win, fmap, qtab,
    terms, starts_all, maps_out,
    pv, qv, wv, send1, recv1, acc, grid, send2, ctab, maps, svec, fv, wdup,
    ld, s1, r1, s2, sx, sp, rt, ss, rs,
):
    me = lax.axis_index("facet")
    c = lax.axis_index("col")
    nx = ncol // 2
    xq, core = lax.div(c, 2), lax.rem(c, 2)
    partner = xq * 2 + 1 - core
    pow2 = nf & (nf - 1) == 0
    blocks = prep.shape[1]
    xa, width = wts.shape[1:]
    half = width // 2
    oc = fmap.shape[0]
    chunks = CHUNKS
    deep = nf <= 8
    step = blocks // chunks

    def peer(i):
        if not pow2:
            return lax.rem(me + i, nf)
        out, b = 0, 1
        while b < nf:
            mb, ib = lax.rem(lax.div(me, b), 2), lax.rem(lax.div(i, b), 2)
            out = out + b * (mb + ib - 2 * mb * ib)
            b *= 2
        return out

    def source(i):
        return peer(i) if pow2 else lax.rem(me + nf - i, nf)

    barrier = pltpu.get_barrier_semaphore()

    @pl.loop(1, nf)
    def _(i):
        pl.semaphore_signal(barrier, inc=1, device_id={"facet": peer(i)}, device_id_type=MESH)

    for i in range(1, ncol):
        pl.semaphore_signal(
            barrier, inc=1, device_id={"col": lax.rem(c + i, ncol)}, device_id_type=MESH
        )

    loads = [
        pltpu.make_async_copy(
            prep.at[:, pl.ds(k * step, step)], pv.at[:, pl.ds(k * step, step)], ld.at[k]
        )
        for k in range(chunks)
    ]
    w_load = pltpu.make_async_copy(wts, wv, ld.at[chunks])
    q_load = pltpu.make_async_copy(qtab, qv, ld.at[chunks + 1])
    f_load = pltpu.make_async_copy(fmap, fv, ld.at[chunks + 2])
    for copy in loads:
        copy.start()
    w_load.start()
    q_load.start()
    f_load.start()

    lane = iota(svec.shape, 1)
    row = jnp.zeros(svec.shape, jnp.int32)
    svec[...] = lax.fori_loop(0, nf, lambda j, v: jnp.where(lane == j, starts[j], v), row)

    def remote(src, dst, send, recv, **where):
        return pltpu.make_async_remote_copy(
            src_ref=src, dst_ref=dst, send_sem=send, recv_sem=recv,
            device_id=where, device_id_type=MESH,
        )

    def send_first(h, j):
        return remote(send1.at[h, j], recv1.at[h, me], s1.at[h, j], r1.at[h, me], facet=j)

    def recv_first(h, j):
        return remote(send1.at[h, j], recv1.at[h, j], s1.at[h, j], r1.at[h, j], facet=j)

    def send_second(h, j):
        return remote(send2.at[h, j], terms.at[c, me, h], s2.at[h, j], rt.at[c, me, h], facet=j)

    def arrival(cc, j, h):
        return remote(send2.at[h, j], terms.at[cc, j, h], s2.at[h, j], rt.at[cc, j, h], facet=j)

    def forward_x(src, j, h, q):
        return remote(
            src, terms.at[c, j, h], sx.at[q, j, h], rt.at[c, j, h],
            col=lax.rem(xq + q, nx) * 2 + core,
        )

    def forward_partner(src, cc, j, h):
        return remote(src, terms.at[cc, j, h], sp.at[cc, j, h], rt.at[cc, j, h], col=partner)

    row_d = iota((XM, 2 * XM), 1) - iota((XM, 2 * XM), 0)
    fwd_table = fwd[...]

    def contribution(j, dst):
        start = starts[j]
        block = lax.div(start, XM)
        shift = lax.rem(start, XM)
        above = lax.rem(block + 1, blocks)
        top = jnp.concatenate([pv[0, block], pv[1, block]], axis=1)
        low = jnp.concatenate([pv[0, above], pv[1, above]], axis=1)
        picked = mm(one_hot(row_d == shift), jnp.concatenate([top, low], axis=0))
        prod = mm(fwd_table, picked.astype(BF16))
        re = prod[:XM, :width] - prod[XM:, width:]
        im = prod[:XM, width:] + prod[XM:, :width]
        first = iota(re.shape, 1) < half
        dst[0, j] = jnp.where(first, re, pltpu.roll(im, half, 1)).astype(BF16)
        dst[1, j] = jnp.where(first, pltpu.roll(re, half, 1), im).astype(BF16)

    for copy in loads:
        copy.wait()
    pl.semaphore_wait(barrier, nf - 1 + ncol - 1)

    @pl.loop(1, nf, unroll=deep)
    def _(i):
        j = peer(nf - i)
        contribution(j, send1)
        send_first(0, j).start()

    @pl.loop(1, nf)
    def _(i):
        send_first(1, peer(nf - i)).start()

    contribution(me, recv1)

    start_sends = []
    for i in range(1, ncol):
        to = lax.rem(c + i, ncol)
        start_sends.append(remote(svec, starts_all.at[c], ss.at[i], rs.at[c], col=to))
        start_sends[-1].start()
    own_starts = pltpu.make_async_copy(svec, starts_all.at[c], ld.at[chunks + 3])
    own_starts.start()

    turn_d = iota((XM, XM), 0) - iota((XM, XM), 1)
    turn_by = lax.rem(starts[me], ALIGN)
    turn = (turn_d == turn_by) | (turn_d == turn_by - XM)
    turned = mm(one_hot(turn), bwd[...]).astype(BF16)
    turned = jnp.concatenate([turned[:, :XM], turned[:, XM:]], axis=0)
    back_d = iota((XM, xa), 1) - iota((XM, xa), 0)

    @pl.loop(0, nf, unroll=deep)
    def _(j):
        hit = (back_d == fac[j]) | (back_d == fac[j] - xa)
        ctab[j] = mm(turned, one_hot(hit)).astype(BF16)

    w_load.wait()
    near = iota((xa, width), 1) < half
    for p in range(2):
        w = wv[p].astype(F32)
        swapped = pltpu.roll(w, half, 1)
        wdup[0, p] = jnp.where(near, w, swapped)
        wdup[1, p] = jnp.where(near, swapped, w)

    grid_d = iota((xa, XM), 0) - iota((xa, XM), 1)

    def place(h, j):
        hit = (grid_d == fac[j]) | (grid_d == fac[j] - xa)
        return mm(one_hot(hit), recv1[h, j])

    def twist(prod, conj):
        n = prod.shape[0] // 2
        crossed = pltpu.roll(prod[n:], half, 1)
        first = iota(crossed.shape, 1) < half
        minus = jnp.logical_not(first) if conj else first
        return prod[:n] + jnp.where(minus, -crossed, crossed)

    def window_maps():
        f_load.wait()
        fm = fv[...]
        col_n = iota((oc, width), 0)
        for k in range(ncol):
            m = lax.dot_general(
                one_hot(col_n == win[k : k + 1, :]), fm, (((0,), (0,)), ((), ())),
                preferred_element_type=F32,
            ).astype(BF16)
            m_re, m_im = m[:, :oc], m[:, oc:]
            upper = jnp.concatenate([m_re, m_im], axis=1)
            lower = jnp.concatenate([-m_im, m_re], axis=1)
            maps[k] = jnp.concatenate(
                [upper[:half], lower[:half], upper[half:], lower[half:]], axis=0
            )

    own_copies = []
    map_copy = pltpu.make_async_copy(maps, maps_out, ld.at[chunks + 4])
    for h in range(2):
        acc[...] = place(h, me)

        @pl.loop(1, nf)
        def _(i):
            j = source(nf - i)
            recv_first(h, j).wait_recv()
            acc[...] += place(h, j)

        if h == 0:
            q_load.wait()
        table = qv[...]
        spectrum = twist(mm(table, acc[...].astype(BF16)), False)
        crossed = wdup[h, 1] * pltpu.roll(spectrum, half, 1)
        weighted = wdup[h, 0] * spectrum + jnp.where(near, -crossed, crossed)
        image = twist(mm(table, weighted.astype(BF16)), True)
        grid[...] = (image * image_gain(nf, xa)).astype(BF16)

        def back(j):
            return twist(mm(ctab[j], grid[...]), False).astype(BF16)

        send2[h, me] = back(me)
        copy = pltpu.make_async_copy(
            send2.at[h, me], terms.at[c, me, h], ld.at[chunks + 5 + h]
        )
        copy.start()
        own_copies.append(copy)
        for q in range(1, nx):
            forward_x(send2.at[h, me], me, h, q).start()
        forward_partner(send2.at[h, me], c, me, h).start()

        @pl.loop(1, nf, unroll=deep)
        def _(i):
            j = peer(nf - i)
            send2[h, j] = back(j)
            send_second(h, j).start()

        if h == 0:
            window_maps()
            map_copy.start()

    def relay(u):
        h, j = lax.div(u, nf), source(nf - lax.rem(u, nf))
        for q in range(1, nx):
            cc = lax.rem(xq + nx - q, nx) * 2 + core
            arrival(cc, j, h).wait_recv()
            forward_partner(terms.at[cc, j, h], cc, j, h).start()

    @pl.loop(0, 2 * nf)
    def _(u):
        h, i = lax.div(u, nf), lax.rem(u, nf)

        @pl.when(i > 0)
        def _():
            j = source(nf - i)
            arrival(c, j, h).wait_recv()
            for q in range(1, nx):
                forward_x(terms.at[c, j, h], j, h, q).start()
            forward_partner(terms.at[c, j, h], c, j, h).start()

        @pl.when(u >= LAG)
        def _():
            relay(u - LAG)

    @pl.loop(2 * nf - LAG, 2 * nf)
    def _(u):
        relay(u)

    for copy in own_copies:
        copy.wait()
    own_starts.wait()
    map_copy.wait()
    for i in range(1, ncol):
        start_sends[i - 1].wait_send()
        frm = lax.rem(c + ncol - i, ncol)
        remote(svec, starts_all.at[frm], ss.at[i], rs.at[frm], col=frm).wait_recv()

    @pl.loop(0, nf)
    def _(j):
        for h in range(2):
            for q in range(nx):
                cc = lax.rem(xq + q, nx) * 2 + 1 - core
                arrival(cc, j, h).wait_recv()
                mine = lax.rem(xq + q, nx) * 2 + core
                forward_partner(terms.at[c, j, h], mine, j, h).wait_send()
            for q in range(1, nx):
                forward_x(terms.at[c, j, h], j, h, q).wait_send()

    @pl.loop(1, nf)
    def _(i):
        j = peer(i)
        for h in range(2):
            send_first(h, j).wait_send()
            send_second(h, j).wait_send()


def image_gain(nf, xa):
    return math.sqrt(nf * XM) / math.sqrt(xa)


def finish_kernel(nf, ncol, starts_all, terms, maps_in, out, tv, acc, maps, stage, tsem, osem):
    c = lax.axis_index("col")
    own_rows = out.shape[1]
    oc = out.shape[2]
    total = own_rows * ncol
    base = c * own_rows
    count = ncol * nf

    def offset(t):
        cc, j = lax.div(t, nf), lax.rem(t, nf)
        rel = starts_all[cc, 0, j] - base + XM
        rel = jnp.where(rel < 0, rel + total, rel)
        rel = jnp.where(rel >= total, rel - total, rel)
        return cc, j, rel

    def fetch(t, cc, j):
        return pltpu.make_async_copy(terms.at[cc, j], tv.at[t], tsem.at[t])

    map_load = pltpu.make_async_copy(maps_in, maps, tsem.at[count])
    map_load.start()

    @pl.loop(0, count)
    def _(t):
        cc, j, rel = offset(t)

        @pl.when(rel < own_rows + XM)
        def _():
            fetch(t, cc, j).start()

    acc[...] = jnp.zeros_like(acc)
    slot = iota((XM, 2 * oc), 0)
    edge = iota((ALIGN, 2 * oc), 0)
    map_load.wait()

    @pl.loop(0, count)
    def _(t):
        cc, j, rel = offset(t)

        @pl.when(rel < own_rows + XM)
        def _():
            fetch(t, cc, j).wait()
            value = mm(jnp.concatenate([tv[t, 0], tv[t, 1]], axis=1), maps[cc])
            turn = lax.rem(rel, ALIGN)
            low = pl.multiple_of(rel - turn, ALIGN)
            acc[pl.ds(low, XM), :] += jnp.where(slot >= turn, value, 0.0)
            acc[pl.ds(pl.multiple_of(low + XM, ALIGN), ALIGN), :] += jnp.where(
                edge < turn, value[:ALIGN], 0.0
            )

    chunk = own_rows // OUT_CHUNKS
    copies = []
    for k in range(OUT_CHUNKS):
        rows = pl.ds(k * chunk, chunk)
        src = pl.ds(XM + k * chunk, chunk)
        stage[0, rows, :] = acc[src, :oc].astype(BF16)
        stage[1, rows, :] = acc[src, oc:].astype(BF16)
        copy = pltpu.make_async_copy(stage.at[:, rows, :], out.at[:, rows, :], osem.at[k])
        copy.start()
        copies.append(copy)
    for copy in copies:
        copy.wait()


def body(prepared, sub_off, fac_off, win_col, vis_weights):
    nf = fac_off.shape[0]
    ncol = lax.axis_size("col")
    facet_strip = prepared[0]
    facet_len, width = facet_strip.shape[1:]
    strip_blocks = facet_strip.reshape(2, facet_len // XM, XM, width)
    weights = vis_weights[0]
    xa = weights.shape[1]
    oc = width * ncol // 2
    own_rows = facet_len // ncol
    starts = sub_off[:, 0]
    lanes = -(-nf // 128) * 128

    forward, backward = window_tables(XM)
    q_table = stacked(*dft(xa, -1.0, 1.0 / math.sqrt(nf * XM)), 0)
    out_map = stacked(*dft(oc, 1.0, 1.0 / math.sqrt(2 * oc)), 1)

    smem = pl.BlockSpec(memory_space=pltpu.SMEM)
    vmem = pl.BlockSpec(memory_space=pltpu.VMEM)
    hbm = pl.BlockSpec(memory_space=pl.ANY)
    dma = pltpu.SemaphoreType.DMA
    halves = pltpu.VMEM((2, nf, XM, width), BF16)
    maps = (ncol, 2 * width, 2 * oc)
    terms, starts_all, maps_all = pl.pallas_call(
        functools.partial(exchange_kernel, nf, ncol),
        out_shape=(
            jax.ShapeDtypeStruct((ncol, nf, 2, XM, width), BF16),
            jax.ShapeDtypeStruct((ncol, 8, lanes), jnp.int32),
            jax.ShapeDtypeStruct(maps, BF16),
        ),
        in_specs=[smem, smem, hbm, hbm, vmem, vmem, vmem, hbm, hbm],
        out_specs=(hbm, hbm, hbm),
        scratch_shapes=[
            pltpu.VMEM(strip_blocks.shape, BF16),
            pltpu.VMEM(q_table.shape, BF16),
            pltpu.VMEM(weights.shape, BF16),
            halves,
            halves,
            pltpu.VMEM((xa, width), F32),
            pltpu.VMEM((xa, width), BF16),
            halves,
            pltpu.VMEM((nf, 2 * XM, xa), BF16),
            pltpu.VMEM(maps, BF16),
            pltpu.VMEM((8, lanes), jnp.int32),
            pltpu.VMEM(out_map.shape, BF16),
            pltpu.VMEM((2, 2, xa, width), F32),
            dma((CHUNKS + 7,)), dma((2, nf)), dma((2, nf)), dma((2, nf)),
            dma((ncol, nf, 2)), dma((ncol, nf, 2)), dma((ncol, nf, 2)), dma((ncol,)), dma((ncol,)),
        ],
        compiler_params=pltpu.CompilerParams(collective_id=0, has_side_effects=True),
        name="exchange",
    )(
        starts, fac_off, strip_blocks, weights, jnp.asarray(forward), jnp.asarray(backward),
        win_col, jnp.asarray(out_map), jnp.asarray(q_table),
    )
    out = pl.pallas_call(
        functools.partial(finish_kernel, nf, ncol),
        out_shape=jax.ShapeDtypeStruct((2, own_rows, oc), BF16),
        in_specs=[smem, hbm, hbm],
        out_specs=hbm,
        scratch_shapes=[
            pltpu.VMEM((ncol * nf, 2, XM, width), BF16),
            pltpu.VMEM((own_rows + 2 * XM + ALIGN, 2 * oc), F32),
            pltpu.VMEM(maps, BF16),
            pltpu.VMEM((2, own_rows, oc), BF16),
            dma((ncol * nf + 1,)),
            dma((OUT_CHUNKS,)),
        ],
        name="finish",
    )(starts_all, terms, maps_all)
    return out[None]


def solution(mesh):
    in_specs = (
        P("facet", None, None, "col"),
        P(None, "col"),
        P(),
        P(),
        P("facet", None, None, "col"),
    )
    out_specs = P("facet", None, "col", None)
    return jax.shard_map(body, mesh=mesh, in_specs=in_specs, out_specs=out_specs, check_vma=False)
```

```python
import functools
import math

import jax
import jax.numpy as jnp
import numpy as np
from jax import lax
from jax.experimental import pallas as pl
from jax.experimental.pallas import tpu as pltpu
from jax.sharding import PartitionSpec as P

XM = 128
ALIGN = 16
CHUNKS = 8
OUT_CHUNKS = 8
LAG = 8
MESH = pl.DeviceIdType.MESH
F32 = jnp.float32
BF16 = jnp.bfloat16


def dft(length, sign, scaling):
    ids = np.arange(length)
    angles = 2.0 * np.pi / length * (ids[:, None] * ids[None, :] % length)
    return np.cos(angles) * scaling, sign * np.sin(angles) * scaling


def stacked(real_part, imag_part, axis):
    return np.concatenate([real_part, imag_part], axis=axis).astype(jnp.bfloat16)


def window_tables(length):
    taper = 0.3 + 0.7 * np.sin(np.pi * (np.arange(length) + 0.5) / length) ** 2
    scaling = 1.0 / math.sqrt(length)
    fwd_re, fwd_im = dft(length, -1.0, scaling)
    back_re, back_im = dft(length, 1.0, scaling)
    forward = stacked(fwd_re * taper[None, :], fwd_im * taper[None, :], 0)
    backward = stacked(back_re * taper[:, None], back_im * taper[:, None], 1)
    return forward, backward


def mm(a, b):
    return jnp.dot(a, b, preferred_element_type=F32)


def iota(shape, dim):
    return lax.broadcasted_iota(jnp.int32, shape, dim)


def one_hot(hit):
    return jnp.where(hit, 1.0, 0.0).astype(BF16)


def exchange_kernel(
    nf, ncol, starts, fac, prep, wts, fwd, bwd, win, fmap, qtab,
    terms, starts_all, maps_out,
    pv, qv, wv, send1, recv1, acc, grid, send2, ctab, maps, svec, fv, wdup,
    ld, s1, r1, s2, sx, sp, rt, ss, rs,
):
    me = lax.axis_index("facet")
    c = lax.axis_index("col")
    nx = ncol // 2
    xq, core = lax.div(c, 2), lax.rem(c, 2)
    partner = xq * 2 + 1 - core
    pow2 = nf & (nf - 1) == 0
    blocks = prep.shape[1]
    xa, width = wts.shape[1:]
    half = width // 2
    oc = fmap.shape[0]
    chunks = CHUNKS
    deep = nf <= 8
    step = blocks // chunks

    def peer(i):
        if not pow2:
            return lax.rem(me + i, nf)
        out, b = 0, 1
        while b < nf:
            mb, ib = lax.rem(lax.div(me, b), 2), lax.rem(lax.div(i, b), 2)
            out = out + b * (mb + ib - 2 * mb * ib)
            b *= 2
        return out

    def source(i):
        return peer(i) if pow2 else lax.rem(me + nf - i, nf)

    barrier = pltpu.get_barrier_semaphore()

    @pl.loop(1, nf)
    def _(i):
        pl.semaphore_signal(barrier, inc=1, device_id={"facet": peer(i)}, device_id_type=MESH)

    for i in range(1, ncol):
        pl.semaphore_signal(
            barrier, inc=1, device_id={"col": lax.rem(c + i, ncol)}, device_id_type=MESH
        )

    loads = [
        pltpu.make_async_copy(
            prep.at[:, pl.ds(k * step, step)], pv.at[:, pl.ds(k * step, step)], ld.at[k]
        )
        for k in range(chunks)
    ]
    w_load = pltpu.make_async_copy(wts, wv, ld.at[chunks])
    q_load = pltpu.make_async_copy(qtab, qv, ld.at[chunks + 1])
    f_load = pltpu.make_async_copy(fmap, fv, ld.at[chunks + 2])
    f_load.start()
    for copy in loads:
        copy.start()
    w_load.start()
    q_load.start()

    lane = iota(svec.shape, 1)
    row = jnp.zeros(svec.shape, jnp.int32)
    svec[...] = lax.fori_loop(0, nf, lambda j, v: jnp.where(lane == j, starts[j], v), row)

    def remote(src, dst, send, recv, **where):
        return pltpu.make_async_remote_copy(
            src_ref=src, dst_ref=dst, send_sem=send, recv_sem=recv,
            device_id=where, device_id_type=MESH,
        )

    def send_first(h, j):
        return remote(send1.at[h, j], recv1.at[h, me], s1.at[h, j], r1.at[h, me], facet=j)

    def recv_first(h, j):
        return remote(send1.at[h, j], recv1.at[h, j], s1.at[h, j], r1.at[h, j], facet=j)

    def send_second(h, j):
        return remote(send2.at[h, j], terms.at[c, me, h], s2.at[h, j], rt.at[c, me, h], facet=j)

    def arrival(cc, j, h):
        return remote(send2.at[h, j], terms.at[cc, j, h], s2.at[h, j], rt.at[cc, j, h], facet=j)

    def forward_x(src, j, h, q):
        return remote(
            src, terms.at[c, j, h], sx.at[q, j, h], rt.at[c, j, h],
            col=lax.rem(xq + q, nx) * 2 + core,
        )

    def forward_partner(src, cc, j, h):
        return remote(src, terms.at[cc, j, h], sp.at[cc, j, h], rt.at[cc, j, h], col=partner)

    row_d = iota((XM, 2 * XM), 1) - iota((XM, 2 * XM), 0)
    fwd_table = fwd[...]

    def contribution(j, dst):
        start = starts[j]
        block = lax.div(start, XM)
        shift = lax.rem(start, XM)
        above = lax.rem(block + 1, blocks)
        top = jnp.concatenate([pv[0, block], pv[1, block]], axis=1)
        low = jnp.concatenate([pv[0, above], pv[1, above]], axis=1)
        picked = mm(one_hot(row_d == shift), jnp.concatenate([top, low], axis=0))
        prod = mm(fwd_table, picked.astype(BF16))
        re = prod[:XM, :width] - prod[XM:, width:]
        im = prod[:XM, width:] + prod[XM:, :width]
        first = iota(re.shape, 1) < half
        dst[0, j] = jnp.where(first, re, pltpu.roll(im, half, 1)).astype(BF16)
        dst[1, j] = jnp.where(first, pltpu.roll(re, half, 1), im).astype(BF16)

    def window_maps():
        f_load.wait()
        fm = fv[...]
        col_n = iota((oc, width), 0)
        for k in range(ncol):
            m = lax.dot_general(
                one_hot(col_n == win[k : k + 1, :]), fm, (((0,), (0,)), ((), ())),
                preferred_element_type=F32,
            ).astype(BF16)
            m_re, m_im = m[:, :oc], m[:, oc:]
            upper = jnp.concatenate([m_re, m_im], axis=1)
            lower = jnp.concatenate([-m_im, m_re], axis=1)
            maps[k] = jnp.concatenate(
                [upper[:half], lower[:half], upper[half:], lower[half:]], axis=0
            )

    map_copy = pltpu.make_async_copy(maps, maps_out, ld.at[chunks + 4])
    window_maps()
    map_copy.start()
    for copy in loads:
        copy.wait()
    pl.semaphore_wait(barrier, nf - 1 + ncol - 1)

    @pl.loop(1, nf, unroll=deep)
    def _(i):
        j = peer(nf - i)
        contribution(j, send1)
        send_first(0, j).start()

    @pl.loop(1, nf)
    def _(i):
        send_first(1, peer(nf - i)).start()

    contribution(me, recv1)

    start_sends = []
    for i in range(1, ncol):
        to = lax.rem(c + i, ncol)
        start_sends.append(remote(svec, starts_all.at[c], ss.at[i], rs.at[c], col=to))
        start_sends[-1].start()
    own_starts = pltpu.make_async_copy(svec, starts_all.at[c], ld.at[chunks + 3])
    own_starts.start()

    turn_d = iota((XM, XM), 0) - iota((XM, XM), 1)
    turn_by = lax.rem(starts[me], ALIGN)
    turn = (turn_d == turn_by) | (turn_d == turn_by - XM)
    turned = mm(one_hot(turn), bwd[...]).astype(BF16)
    turned = jnp.concatenate([turned[:, :XM], turned[:, XM:]], axis=0)
    back_d = iota((XM, xa), 1) - iota((XM, xa), 0)

    @pl.loop(0, nf, unroll=deep)
    def _(j):
        hit = (back_d == fac[j]) | (back_d == fac[j] - xa)
        ctab[j] = mm(turned, one_hot(hit)).astype(BF16)

    w_load.wait()
    near = iota((xa, width), 1) < half
    for p in range(2):
        w = wv[p].astype(F32)
        swapped = pltpu.roll(w, half, 1)
        wdup[0, p] = jnp.where(near, w, swapped)
        wdup[1, p] = jnp.where(near, swapped, w)

    grid_d = iota((xa, XM), 0) - iota((xa, XM), 1)

    def place(h, j):
        hit = (grid_d == fac[j]) | (grid_d == fac[j] - xa)
        return mm(one_hot(hit), recv1[h, j])

    def twist(prod, conj):
        n = prod.shape[0] // 2
        crossed = pltpu.roll(prod[n:], half, 1)
        first = iota(crossed.shape, 1) < half
        minus = jnp.logical_not(first) if conj else first
        return prod[:n] + jnp.where(minus, -crossed, crossed)

    own_copies = []
    for h in range(2):
        acc[...] = place(h, me)

        @pl.loop(1, nf)
        def _(i):
            j = source(nf - i)
            recv_first(h, j).wait_recv()
            acc[...] += place(h, j)

        if h == 0:
            q_load.wait()
        table = qv[...]
        spectrum = twist(mm(table, acc[...].astype(BF16)), False)
        crossed = wdup[h, 1] * pltpu.roll(spectrum, half, 1)
        weighted = wdup[h, 0] * spectrum + jnp.where(near, -crossed, crossed)
        image = twist(mm(table, weighted.astype(BF16)), True)
        grid[...] = (image * image_gain(nf, xa)).astype(BF16)

        def back(j):
            return twist(mm(ctab[j], grid[...]), False).astype(BF16)

        send2[h, me] = back(me)
        copy = pltpu.make_async_copy(
            send2.at[h, me], terms.at[c, me, h], ld.at[chunks + 5 + h]
        )
        copy.start()
        own_copies.append(copy)
        for q in range(1, nx):
            forward_x(send2.at[h, me], me, h, q).start()
        forward_partner(send2.at[h, me], c, me, h).start()

        @pl.loop(1, nf, unroll=deep)
        def _(i):
            j = peer(i)
            send2[h, j] = back(j)
            send_second(h, j).start()

    def relay(u):
        h, j = lax.div(u, nf), source(lax.rem(u, nf))
        for q in range(1, nx):
            cc = lax.rem(xq + nx - q, nx) * 2 + core
            arrival(cc, j, h).wait_recv()
            forward_partner(terms.at[cc, j, h], cc, j, h).start()

    @pl.loop(0, 2 * nf)
    def _(u):
        h, i = lax.div(u, nf), lax.rem(u, nf)

        @pl.when(i > 0)
        def _():
            j = source(i)
            arrival(c, j, h).wait_recv()
            for q in range(1, nx):
                forward_x(terms.at[c, j, h], j, h, q).start()
            forward_partner(terms.at[c, j, h], c, j, h).start()

        @pl.when(u >= LAG)
        def _():
            relay(u - LAG)

    @pl.loop(2 * nf - LAG, 2 * nf)
    def _(u):
        relay(u)

    for copy in own_copies:
        copy.wait()
    own_starts.wait()
    map_copy.wait()
    for i in range(1, ncol):
        start_sends[i - 1].wait_send()
        frm = lax.rem(c + ncol - i, ncol)
        remote(svec, starts_all.at[frm], ss.at[i], rs.at[frm], col=frm).wait_recv()

    @pl.loop(0, nf)
    def _(j):
        for h in range(2):
            for q in range(nx):
                cc = lax.rem(xq + q, nx) * 2 + 1 - core
                arrival(cc, j, h).wait_recv()
                mine = lax.rem(xq + q, nx) * 2 + core
                forward_partner(terms.at[c, j, h], mine, j, h).wait_send()
            for q in range(1, nx):
                forward_x(terms.at[c, j, h], j, h, q).wait_send()

    @pl.loop(1, nf)
    def _(i):
        j = peer(i)
        for h in range(2):
            send_first(h, j).wait_send()
            send_second(h, j).wait_send()


def image_gain(nf, xa):
    return math.sqrt(nf * XM) / math.sqrt(xa)


def finish_kernel(nf, ncol, starts_all, terms, maps_in, out, tv, acc, maps, stage, tsem, osem):
    c = lax.axis_index("col")
    own_rows = out.shape[1]
    oc = out.shape[2]
    total = own_rows * ncol
    base = c * own_rows
    count = ncol * nf

    def offset(t):
        cc, j = lax.div(t, nf), lax.rem(t, nf)
        rel = starts_all[cc, 0, j] - base + XM
        rel = jnp.where(rel < 0, rel + total, rel)
        rel = jnp.where(rel >= total, rel - total, rel)
        return cc, j, rel

    def fetch(t, cc, j):
        return pltpu.make_async_copy(terms.at[cc, j], tv.at[t], tsem.at[t])

    map_load = pltpu.make_async_copy(maps_in, maps, tsem.at[count])
    map_load.start()

    @pl.loop(0, count)
    def _(t):
        cc, j, rel = offset(t)

        @pl.when(rel < own_rows + XM)
        def _():
            fetch(t, cc, j).start()

    acc[...] = jnp.zeros_like(acc)
    slot = iota((XM, 2 * oc), 0)
    edge = iota((ALIGN, 2 * oc), 0)
    map_load.wait()

    @pl.loop(0, count)
    def _(t):
        cc, j, rel = offset(t)

        @pl.when(rel < own_rows + XM)
        def _():
            fetch(t, cc, j).wait()
            value = mm(jnp.concatenate([tv[t, 0], tv[t, 1]], axis=1), maps[cc])
            turn = lax.rem(rel, ALIGN)
            low = pl.multiple_of(rel - turn, ALIGN)
            acc[pl.ds(low, XM), :] += jnp.where(slot >= turn, value, 0.0)
            acc[pl.ds(pl.multiple_of(low + XM, ALIGN), ALIGN), :] += jnp.where(
                edge < turn, value[:ALIGN], 0.0
            )

    chunk = own_rows // OUT_CHUNKS
    copies = []
    for k in range(OUT_CHUNKS):
        rows = pl.ds(k * chunk, chunk)
        src = pl.ds(XM + k * chunk, chunk)
        stage[0, rows, :] = acc[src, :oc].astype(BF16)
        stage[1, rows, :] = acc[src, oc:].astype(BF16)
        copy = pltpu.make_async_copy(stage.at[:, rows, :], out.at[:, rows, :], osem.at[k])
        copy.start()
        copies.append(copy)
    for copy in copies:
        copy.wait()


def body(prepared, sub_off, fac_off, win_col, vis_weights):
    nf = fac_off.shape[0]
    ncol = lax.axis_size("col")
    facet_strip = prepared[0]
    facet_len, width = facet_strip.shape[1:]
    strip_blocks = facet_strip.reshape(2, facet_len // XM, XM, width)
    weights = vis_weights[0]
    xa = weights.shape[1]
    oc = width * ncol // 2
    own_rows = facet_len // ncol
    starts = sub_off[:, 0]
    lanes = -(-nf // 128) * 128

    forward, backward = window_tables(XM)
    q_table = stacked(*dft(xa, -1.0, 1.0 / math.sqrt(nf * XM)), 0)
    out_map = stacked(*dft(oc, 1.0, 1.0 / math.sqrt(2 * oc)), 1)

    smem = pl.BlockSpec(memory_space=pltpu.SMEM)
    vmem = pl.BlockSpec(memory_space=pltpu.VMEM)
    hbm = pl.BlockSpec(memory_space=pl.ANY)
    dma = pltpu.SemaphoreType.DMA
    halves = pltpu.VMEM((2, nf, XM, width), BF16)
    maps = (ncol, 2 * width, 2 * oc)
    terms, starts_all, maps_all = pl.pallas_call(
        functools.partial(exchange_kernel, nf, ncol),
        out_shape=(
            jax.ShapeDtypeStruct((ncol, nf, 2, XM, width), BF16),
            jax.ShapeDtypeStruct((ncol, 8, lanes), jnp.int32),
            jax.ShapeDtypeStruct(maps, BF16),
        ),
        in_specs=[smem, smem, hbm, hbm, vmem, vmem, vmem, hbm, hbm],
        out_specs=(hbm, hbm, hbm),
        scratch_shapes=[
            pltpu.VMEM(strip_blocks.shape, BF16),
            pltpu.VMEM(q_table.shape, BF16),
            pltpu.VMEM(weights.shape, BF16),
            halves,
            halves,
            pltpu.VMEM((xa, width), F32),
            pltpu.VMEM((xa, width), BF16),
            halves,
            pltpu.VMEM((nf, 2 * XM, xa), BF16),
            pltpu.VMEM(maps, BF16),
            pltpu.VMEM((8, lanes), jnp.int32),
            pltpu.VMEM(out_map.shape, BF16),
            pltpu.VMEM((2, 2, xa, width), F32),
            dma((CHUNKS + 7,)), dma((2, nf)), dma((2, nf)), dma((2, nf)),
            dma((ncol, nf, 2)), dma((ncol, nf, 2)), dma((ncol, nf, 2)), dma((ncol,)), dma((ncol,)),
        ],
        compiler_params=pltpu.CompilerParams(collective_id=0, has_side_effects=True),
        name="exchange",
    )(
        starts, fac_off, strip_blocks, weights, jnp.asarray(forward), jnp.asarray(backward),
        win_col, jnp.asarray(out_map), jnp.asarray(q_table),
    )
    out = pl.pallas_call(
        functools.partial(finish_kernel, nf, ncol),
        out_shape=jax.ShapeDtypeStruct((2, own_rows, oc), BF16),
        in_specs=[smem, hbm, hbm],
        out_specs=hbm,
        scratch_shapes=[
            pltpu.VMEM((ncol * nf, 2, XM, width), BF16),
            pltpu.VMEM((own_rows + 2 * XM + ALIGN, 2 * oc), F32),
            pltpu.VMEM(maps, BF16),
            pltpu.VMEM((2, own_rows, oc), BF16),
            dma((ncol * nf + 1,)),
            dma((OUT_CHUNKS,)),
        ],
        name="finish",
    )(starts_all, terms, maps_all)
    return out[None]


def solution(mesh):
    in_specs = (
        P("facet", None, None, "col"),
        P(None, "col"),
        P(),
        P(),
        P("facet", None, None, "col"),
    )
    out_specs = P("facet", None, "col", None)
    return jax.shard_map(body, mesh=mesh, in_specs=in_specs, out_specs=out_specs, check_vma=False)
```
